32 devices in a mesh: gx: 8 (over z, y), gy: 4 (over x, core).
Axes of the slice: x: 2, y: 2, z: 4, core: 2. Of those that a mesh axis runs over, the one named last changes fastest.
Arguments:
- positions: float32 [3, 64, 32, 128], P(None, 'gx', 'gy'), may hold values from 0 to 12
- charges: float32 [64, 32, 128], P('gx', 'gy'), may hold values from -4 to 4
- cell_index: int32 [64, 32, 128], P('gx', 'gy'), may hold values from 0 to 32767, as said below
- task_patch: int32 [8, 4, 32], P('gx', 'gy'), may hold values from 0 to 63
- task_near: int32 [8, 4, 32], P('gx', 'gy'), may hold values from 0 to 8
- task_count: int32 [8, 4], P('gx', 'gy'), may hold values from 1 to 32, as said below
Outputs:
- forces: float32 [3, 64, 32, 128], P(None, 'gx', 'gy')
- recip_potential: float32 [64, 32, 128], P('gx', 'gy')
The draws below stay inside these ranges and needn't reach their ends.
Inputs may be any that keep to these rules, and one draw needn't show every extreme that they name: `task_near`: code k names the neighbouring patch at offset (k // 3 - 1, k % 3 - 1) along the two patch dimensions; only slots below task_count are read. `task_patch`: only slots below task_count are read. `task_count`: in each gx row one device has 32 live tasks, and the counts of the devices that share a gx index sum to at most 4 * 16. Each atom lies in the cell that cell_index names: for an atom of local patch row r and column s with coordinates (a, b, e), the cell has z = floor(e * 256 / 12), x = (r * 4 + floor(a * 4 / 12)) // 8, y = (s * 32 + floor(b * 32 / 12)) // 8, and c = (z * 4 + x) * 32 + y.
All inputs are finite; a program needn't handle non-finite values.
Results may differ from the reference program's by a relative error of at most 0.0003.
Values sent between devices are 32-bit elements; how exact they have to be, the bound alone decides.
No kernel may reach another device: no remote copies, remote signals or barrier semaphores. Data moves between devices by JAX's collectives and lax.ppermute only.
A program may use at most 64 MiB of HBM per device.

```python
import math
import jax
import jax.numpy as jnp
from jax import lax

PX = 8
PY = 8
APATCH = 128
HOSTCAP = 16
TMAX = 32
XR = 4
YC = 32
GZ = 256
GX = 32
GY = 128
NPX = 64
NPY = 32
N_GX = 8
N_GY = 4


def draw_task_count(key, part):
    first_key = jax.random.fold_in(key, 11)
    second_key = jax.random.fold_in(key, 23)
    busiest = jax.random.randint(first_key, (N_GX,), 0, N_GY)
    ceiling = (N_GY * HOSTCAP - 2 * HOSTCAP) // (N_GY - 1)
    lighter = jax.random.randint(second_key, (N_GX, N_GY), 1, ceiling + 1)
    column = jnp.arange(N_GY, dtype=jnp.int32)[None, :]
    return jnp.where(column == busiest[:, None], 2 * HOSTCAP, lighter).astype(jnp.int32)


def atom_layout(key):
    shape = (NPX, NPY, APATCH)
    fine_x = jax.random.randint(jax.random.fold_in(key, 101), shape, 0, XR)
    fine_y = jax.random.randint(jax.random.fold_in(key, 103), shape, 0, YC)
    fine_z = jax.random.randint(jax.random.fold_in(key, 107), shape, 0, GZ)
    fraction = jax.random.uniform(jax.random.fold_in(key, 109), (3,) + shape, jnp.float32)
    return (fine_x, fine_y, fine_z, fraction)


def draw_positions(key, part):
    fine_x, fine_y, fine_z, fraction = atom_layout(key)
    coord_x = (fine_x.astype(jnp.float32) + fraction[0]) * (12.0 / XR)
    coord_y = (fine_y.astype(jnp.float32) + fraction[1]) * (12.0 / YC)
    coord_z = (fine_z.astype(jnp.float32) + fraction[2]) * (12.0 / GZ)
    return jnp.stack([coord_x, coord_y, coord_z]).astype(jnp.float32)


def draw_cell_index(key, part):
    fine_x, fine_y, fine_z, fraction = atom_layout(key)
    local_row = (jnp.arange(NPX, dtype=jnp.int32) % PX)[:, None, None]
    local_col = (jnp.arange(NPY, dtype=jnp.int32) % PY)[None, :, None]
    cell_x = (local_row * XR + fine_x) // PX
    cell_y = (local_col * YC + fine_y) // PY
    return (fine_z * (XR * YC) + cell_x * YC + cell_y).astype(jnp.int32)


def place_ends(drawn, key, low, high):
    dims = drawn.shape
    index_at = [jax.random.randint(jax.random.fold_in(key, axis), (), 0, dims[axis]) for axis in range(len(dims))]
    drawn = drawn.at[tuple(index_at)].set(low)
    longest = dims.index(max(dims))
    index_at[longest] = (index_at[longest] + 1) % dims[longest]
    return drawn.at[tuple(index_at)].set(high)


def levels(own_key, extent, cuts, least, high):
    level = 1.0
    for dim, shards_of in cuts:
        steps = jax.random.uniform(jax.random.fold_in(jax.random.fold_in(own_key, 6), dim), (shards_of,), jnp.float32, least / len(cuts), high / len(cuts))
        level = level * jnp.repeat(jnp.exp(steps), extent[dim] // shards_of).reshape((-1,) + (1,) * (len(extent) - 1 - dim))
    return level


def bell_draw(rng, extent, deviation, reach, shards=(), held_as=jnp.bfloat16):
    values = jax.random.normal(rng, extent, jnp.float32) * deviation
    if len(shards) > 0:
        values = levels(rng, extent, shards, -0.22, 0.18) * values
    return jnp.clip(values, min=-reach, max=reach).astype(held_as)


def setup_inputs(seed: int = 0) -> dict:
    arg_keys = jax.random.split(jax.random.key(seed), 7)
    positions = draw_positions(jax.random.fold_in(arg_keys[6], 71), 0)
    charges = bell_draw(arg_keys[1], (NPX, NPY, APATCH), 1.0, 4.0, ((0, 8), (1, 4)), jnp.float32)
    cell_index = draw_cell_index(jax.random.fold_in(arg_keys[6], 71), 0)
    task_patch = place_ends(jax.random.randint(arg_keys[3], (N_GX, N_GY, TMAX), 0, PX * PY), jax.random.fold_in(arg_keys[3], 1), 0, (PX * PY) - 1).astype(jnp.int32)
    task_near = place_ends(jax.random.randint(arg_keys[4], (N_GX, N_GY, TMAX), 0, 9), jax.random.fold_in(arg_keys[4], 1), 0, 8).astype(jnp.int32)
    task_count = draw_task_count(jax.random.fold_in(arg_keys[6], 71), 0)
    return {"positions": positions, "charges": charges, "cell_index": cell_index, "task_patch": task_patch, "task_near": task_near, "task_count": task_count}


SCREEN = 72.0
PATCH_SIDE = 12.0
KERNEL_SCALE = 64.0


def pair_force(first, second):
    delta = first[:3, :, None] - second[:3, None, :]
    dist_sq = jnp.sum(delta * delta, axis=0)
    strength = jnp.exp(-dist_sq / SCREEN) * (dist_sq + 1.0) ** (-1.5)
    weight = first[3][:, None] * second[3][None, :] * strength
    return jnp.sum(weight[None] * delta, axis=2)


def task_inputs(halo, patch, near):
    rows = halo.shape[1] - 2
    cols = halo.shape[2] - 2
    flat = halo.reshape(4, (rows + 2) * (cols + 2), halo.shape[3])
    prow = patch // cols + 1
    pcol = patch % cols + 1
    drow = near // 3 - 1
    dcol = near % 3 - 1
    first = jnp.take(flat, prow * (cols + 2) + pcol, axis=1)
    second = jnp.take(flat, (prow + drow) * (cols + 2) + pcol + dcol, axis=1)
    zeros = jnp.zeros(patch.shape, jnp.float32)
    shift = jnp.stack([drow.astype(jnp.float32) * PATCH_SIDE, dcol.astype(jnp.float32) * PATCH_SIDE, zeros, zeros])
    second = second + shift[:, :, None]
    return jnp.moveaxis(first, 1, 0), jnp.moveaxis(second, 1, 0)


def patch_sum(per_task_force, patch, live, rows, cols):
    indicator_matrix = ((patch[:, None] == jnp.arange(rows * cols, dtype=jnp.int32)[None, :]) & live[:, None]).astype(jnp.float32)
    accumulated_sum = jnp.einsum("ew,esh->swh", indicator_matrix, per_task_force, precision=lax.Precision.HIGHEST)
    return accumulated_sum.reshape(3, rows, cols, per_task_force.shape[2])


def local_forces(halo, patch, near, count):
    rows = halo.shape[1] - 2
    cols = halo.shape[2] - 2
    live = jnp.arange(patch.shape[0], dtype=jnp.int32) < count
    first, second = task_inputs(halo, patch, near)
    per_task_force = jax.vmap(pair_force)(first, second)
    return patch_sum(per_task_force, patch, live, rows, cols)


def cas_table(length):
    steps = jnp.arange(length, dtype=jnp.int32)
    product = (steps[:, None] * steps[None, :]) % length
    angle = (2.0 * math.pi / length) * product.astype(jnp.float32)
    return jnp.cos(angle) + jnp.sin(angle)


def wave_part(freq, length):
    folded = jnp.minimum(freq, length - freq).astype(jnp.float32) / length
    return folded * folded


def influence(depth_freq, row_freq, column_freq, depth_len, row_len, column_len):
    wave_sq = wave_part(depth_freq, depth_len)[:, None, None] + wave_part(row_freq, row_len)[None, :, None] + wave_part(column_freq, column_len)[None, None, :]
    safe = jnp.where(wave_sq > 0, wave_sq, 1.0)
    return jnp.where(wave_sq > 0, 1.0 / (KERNEL_SCALE * safe), 0.0)


def reference(positions, charges, cell_index, task_patch, task_near, task_count):
    atoms = jnp.concatenate([positions, charges[None]], axis=0)
    padded = jnp.pad(atoms, ((0, 0), (1, 1), (1, 1), (0, 0)), mode="wrap")
    devices = N_GX * N_GY
    patches = task_patch.reshape(devices, -1)
    nears = task_near.reshape(devices, -1)
    counts = task_count.reshape(devices)

    def single_device_path(index):
        row = (index // N_GY).astype(jnp.int32)
        col = (index % N_GY).astype(jnp.int32)
        start = (jnp.zeros((), jnp.int32), row * PX, col * PY, jnp.zeros((), jnp.int32))
        block = lax.dynamic_slice(padded, start, (4, PX + 2, PY + 2, APATCH))
        return local_forces(block, patches[index], nears[index], counts[index])

    parts = lax.map(single_device_path, jnp.arange(devices, dtype=jnp.int32))
    forces = parts.reshape(N_GX, N_GY, 3, PX, PY, APATCH).transpose(2, 0, 3, 1, 4, 5).reshape(3, NPX, NPY, APATCH)

    prow = (jnp.arange(NPX, dtype=jnp.int32) // PX)[:, None, None]
    pcol = (jnp.arange(NPY, dtype=jnp.int32) // PY)[None, :, None]
    plane = cell_index // (XR * YC)
    xrow = prow * XR + (cell_index // YC) % XR
    ycol = pcol * YC + cell_index % YC
    grid = jnp.zeros((GZ, GX, GY), jnp.float32).at[plane, xrow, ycol].add(charges)
    cas_x = cas_table(GX)
    cas_y = cas_table(GY)
    cas_z = cas_table(GZ)
    high = lax.Precision.HIGHEST
    spectrum = jnp.einsum("zxy,zn->nxy", grid, cas_z, precision=high)
    spectrum = jnp.einsum("zxy,yk->zxk", spectrum, cas_y, precision=high)
    spectrum = jnp.einsum("zxk,xm->zmk", spectrum, cas_x, precision=high)
    kernel = influence(jnp.arange(GZ, dtype=jnp.int32), jnp.arange(GX, dtype=jnp.int32), jnp.arange(GY, dtype=jnp.int32), GZ, GX, GY)
    scaled = spectrum * kernel
    field = jnp.einsum("zmk,mx->zxk", scaled, cas_x, precision=high)
    field = jnp.einsum("zxk,ky->zxy", field, cas_y, precision=high)
    field = jnp.einsum("nxy,nz->zxy", field, cas_z, precision=high) / (GX * GY * GZ)
    recip_potential = field[plane, xrow, ycol]
    return forces, recip_potential
```

```python
import math

import jax
import jax.numpy as jnp
import numpy as np
from jax import lax
from jax.experimental import pallas as pl
from jax.experimental.pallas import tpu as pltpu
from jax.sharding import PartitionSpec as P

XR = 4
YC = 32
GZ = 256

SCREEN = 72.0
PATCH_SIDE = 12.0
KERNEL_SCALE = 64.0
SUBLANES = 8
BOTH = ("gx", "gy")


def with_halo(value, sides, width):
    for axis, dim in sides:
        count, length = (lax.axis_size(axis), value.shape[dim])
        up = [(i, (i + 1) % count) for i in range(count)]
        down = [(j, i) for i, j in up]
        last = lax.slice_in_dim(value, length - width, length, axis=dim)
        initial = lax.slice_in_dim(value, 0, width, axis=dim)
        before = lax.ppermute(last, axis, up)
        after = lax.ppermute(initial, axis, down)
        value = jnp.concatenate([before, value, after], axis=dim)
    return value


def cas_numpy(length):
    steps = np.arange(length)
    angle = (2.0 * math.pi / length) * ((steps[:, None] * steps[None, :]) % length)
    return np.cos(angle) + np.sin(angle)


def two_parts(table):
    table = np.asarray(table, np.float32)
    high = table.astype(jnp.bfloat16)
    low = (table - high.astype(np.float32)).astype(jnp.bfloat16)
    return high, low


def split(value):
    high = value.astype(jnp.bfloat16)
    low = (value - high.astype(jnp.float32)).astype(jnp.bfloat16)
    return high, low


def mm(left, right):
    return jnp.dot(left, right, preferred_element_type=jnp.float32)


def mm_lanes(left, right):
    return lax.dot_general(
        left, right, (((1,), (1,)), ((), ())), preferred_element_type=jnp.float32
    )


def force_kernel(patch_ref, near_ref, count_ref, halo_ref, out_ref, *, cols):
    lanes = halo_ref.shape[2]
    out_ref[...] = jnp.zeros_like(out_ref)

    def task(t, carry):
        patch = patch_ref[t]
        near = near_ref[t]
        drow = near // 3 - 1
        dcol = near % 3 - 1
        home = (patch // cols + 1) * (cols + 2) + patch % cols + 1
        away = home + drow * (cols + 2) + dcol
        first = [halo_ref[c, pl.ds(home, SUBLANES, stride=0), :] for c in range(4)]
        second = [halo_ref[c, pl.ds(away, SUBLANES, stride=0), :] for c in range(4)]
        second[0] = second[0] + drow.astype(jnp.float32) * PATCH_SIDE
        second[1] = second[1] + dcol.astype(jnp.float32) * PATCH_SIDE
        base = [pltpu.roll(v, 0, 1, stride=1, stride_axis=0) for v in second]
        sums = [jnp.zeros((SUBLANES, lanes), jnp.float32) for _ in range(3)]
        for j in range(lanes // SUBLANES):
            other = base if j == 0 else [pltpu.roll(v, j * SUBLANES, 1) for v in base]
            delta = [first[c] - other[c] for c in range(3)]
            dist_sq = delta[0] * delta[0] + delta[1] * delta[1] + delta[2] * delta[2]
            root = lax.rsqrt(dist_sq + 1.0)
            weight = other[3] * jnp.exp(dist_sq * (-1.0 / SCREEN)) * (root * root * root)
            sums = [sums[c] + weight * delta[c] for c in range(3)]
        for c in range(3):
            total = jnp.sum(sums[c], axis=0, keepdims=True) * first[3][:1]
            out_ref[c, pl.ds(patch, 1), :] = out_ref[c, pl.ds(patch, 1), :] + total
        return carry

    lax.fori_loop(0, count_ref[0], task, 0)


def pair_forces(halo, patch, near, count):
    rows, cols, atoms = halo.shape[1] - 2, halo.shape[2] - 2, halo.shape[3]
    flat = halo.reshape(4, (rows + 2) * (cols + 2), atoms)
    smem = pl.BlockSpec(memory_space=pltpu.SMEM)
    vmem = pl.BlockSpec(memory_space=pltpu.VMEM)
    out = pl.pallas_call(
        lambda *refs: force_kernel(*refs, cols=cols),
        out_shape=jax.ShapeDtypeStruct((3, rows * cols, atoms), jnp.float32),
        in_specs=[smem, smem, smem, vmem],
        out_specs=vmem,
        name="pair_forces",
    )(patch, near, count, flat)
    return out.reshape(3, rows, cols, atoms)


def cell_parts(cells, block_cells):
    plane = lax.div(cells, jnp.int32(block_cells))
    return plane, cells - plane * block_cells


def strips(rows, cols):
    deep = rows // XR
    wide = SUBLANES // (YC // cols)
    for strip in range(XR * YC // SUBLANES):
        x, part = divmod(strip, YC // SUBLANES)
        yield strip, [
            (x * deep + a, part * wide + b) for a in range(deep) for b in range(wide)
        ]


def strayed(flat, rows, cols):
    deep = rows // XR
    wide = SUBLANES // (YC // cols)
    row = lax.broadcasted_iota(jnp.int32, flat.shape, 0)
    col = lax.broadcasted_iota(jnp.int32, flat.shape, 1)
    own = lax.div(row, jnp.int32(deep)) * (YC // SUBLANES) + lax.div(col, jnp.int32(wide))
    return jnp.max((lax.div(flat, jnp.int32(SUBLANES)) != own).astype(jnp.int32))


def gather_lanes(value, places):
    return jnp.concatenate([value[r, s : s + 1, :] for r, s in places], axis=1)


def onehot_rows(index, count):
    shape = (count, index.shape[1])
    return (lax.broadcasted_iota(jnp.int32, shape, 0) == index).astype(jnp.bfloat16)


def charge_rows(index, charge, count):
    shape = (count, index.shape[1])
    here = lax.broadcasted_iota(jnp.int32, shape, 0) == index
    high, low = split(jnp.where(here, charge, 0.0))
    return jnp.concatenate([high, low], axis=0)


def spread_kernel(charge_ref, cell_ref, cas_ref, out_ref, grid_ref, flat_ref, plane_ref):
    rows, cols, _ = charge_ref.shape
    block = out_ref.shape[1]
    depth = out_ref.shape[0]
    charge = charge_ref[...]
    plane, flat = cell_parts(cell_ref[...], block)
    for strip, places in strips(rows, cols):
        index = gather_lanes(flat, places) - strip * SUBLANES
        lines = charge_rows(index, gather_lanes(charge, places), SUBLANES)
        both = mm_lanes(lines, onehot_rows(gather_lanes(plane, places), depth))
        grid_ref[strip * SUBLANES : (strip + 1) * SUBLANES, :] = (
            both[:SUBLANES] + both[SUBLANES:]
        )

    @pl.when(strayed(flat, rows, cols) > 0)
    def _():
        plane_ref[...] = plane.reshape(plane_ref.shape)
        flat_ref[...] = flat.reshape(flat_ref.shape)
        grid_ref[...] = jnp.zeros_like(grid_ref)

        def patch(p, carry):
            row, col = lax.div(p, jnp.int32(cols)), lax.rem(p, jnp.int32(cols))
            lines = charge_rows(
                flat_ref[pl.ds(p, 1), :], charge_ref[row, pl.ds(col, 1), :], block
            )
            both = mm_lanes(lines, onehot_rows(plane_ref[pl.ds(p, 1), :], depth))
            grid_ref[...] = grid_ref[...] + both[:block] + both[block:]
            return carry

        lax.fori_loop(0, rows * cols, patch, 0)

    high, low = split(grid_ref[...])
    twice = mm_lanes(cas_ref[...], high)
    out_ref[...] = twice[:depth] + twice[depth:] + mm_lanes(cas_ref[:depth], low)


def spread_planes(charges, cells, cas_z):
    rows, cols, atoms = charges.shape
    vmem = pl.BlockSpec(memory_space=pltpu.VMEM)
    return pl.pallas_call(
        spread_kernel,
        out_shape=jax.ShapeDtypeStruct((GZ, XR * YC), jnp.float32),
        in_specs=[vmem] * 3,
        out_specs=vmem,
        scratch_shapes=[
            pltpu.VMEM((XR * YC, GZ), jnp.float32),
            pltpu.VMEM((rows * cols, atoms), jnp.int32),
            pltpu.VMEM((rows * cols, atoms), jnp.int32),
        ],
        name="spread",
    )(charges, cells, cas_z)


def sample_kernel(planes_ref, cell_ref, cas_ref, out_ref, field_ref, flat_ref, plane_ref):
    rows, cols, _ = cell_ref.shape
    depth, block = planes_ref.shape
    plane, flat = cell_parts(cell_ref[...], block)
    high, low = split(planes_ref[...].T)
    pair = mm(jnp.concatenate([high, low], axis=0), cas_ref[:depth])
    field = pair[:block] + pair[block:] + mm(high, cas_ref[depth:])
    field_high, field_low = split(field)
    for strip, places in strips(rows, cols):
        span = slice(strip * SUBLANES, (strip + 1) * SUBLANES)
        lines = jnp.concatenate([field_high[span], field_low[span]], axis=0)
        both = mm(lines, onehot_rows(gather_lanes(plane, places), depth))
        value = both[:SUBLANES] + both[SUBLANES:]
        index = gather_lanes(flat, places) - strip * SUBLANES
        here = lax.broadcasted_iota(jnp.int32, value.shape, 0) == index
        found = jnp.sum(jnp.where(here, value, 0.0), axis=0, keepdims=True)
        atoms = out_ref.shape[2]
        for k, (r, s) in enumerate(places):
            out_ref[r, s : s + 1, :] = found[:, k * atoms : (k + 1) * atoms]

    @pl.when(strayed(flat, rows, cols) > 0)
    def _():
        plane_ref[...] = plane.reshape(plane_ref.shape)
        flat_ref[...] = flat.reshape(flat_ref.shape)
        field_ref[:block, :] = field_high
        field_ref[block:, :] = field_low

        def patch(p, carry):
            row, col = lax.div(p, jnp.int32(cols)), lax.rem(p, jnp.int32(cols))
            both = mm(field_ref[...], onehot_rows(plane_ref[pl.ds(p, 1), :], depth))
            value = both[:block] + both[block:]
            here = lax.broadcasted_iota(jnp.int32, value.shape, 0) == flat_ref[pl.ds(p, 1), :]
            out_ref[row, pl.ds(col, 1), :] = jnp.sum(
                jnp.where(here, value, 0.0), axis=0, keepdims=True
            )
            return carry

        lax.fori_loop(0, rows * cols, patch, 0)


def sample_planes(planes, cells, cas_z):
    rows, cols, atoms = cells.shape
    vmem = pl.BlockSpec(memory_space=pltpu.VMEM)
    return pl.pallas_call(
        sample_kernel,
        out_shape=jax.ShapeDtypeStruct(cells.shape, jnp.float32),
        in_specs=[vmem] * 3,
        out_specs=vmem,
        scratch_shapes=[
            pltpu.VMEM((2 * XR * YC, GZ), jnp.bfloat16),
            pltpu.VMEM((rows * cols, atoms), jnp.int32),
            pltpu.VMEM((rows * cols, atoms), jnp.int32),
        ],
        name="sample",
    )(planes, cells, cas_z)


def wave_part(freq, length):
    folded = jnp.minimum(freq, length - freq).astype(jnp.float32) / length
    return folded * folded


def influence(depth_freq, row_freq, column_freq, depth_len, row_len, column_len):
    wave_sq = (
        wave_part(depth_freq, depth_len)[:, None, None]
        + wave_part(row_freq, row_len)[None, :, None]
        + wave_part(column_freq, column_len)[None, None, :]
    )
    safe = jnp.where(wave_sq > 0, wave_sq, 1.0)
    return jnp.where(wave_sq > 0, 1.0 / (KERNEL_SCALE * safe), 0.0)


def plane_tables(n_x, n_y, share):
    total_x, total_y = n_x * XR, n_y * YC
    cas_x, cas_y = cas_numpy(total_x), cas_numpy(total_y)
    along_y = np.repeat(cas_y.reshape(n_y, 1, YC, total_y), XR, axis=1)
    along_y = along_y.reshape(n_y * XR * YC, total_y)
    to_m = cas_x.reshape(n_x, XR, total_x).transpose(2, 1, 0)
    to_m = np.einsum("mxi,ab->maxib", to_m, np.eye(share))
    to_m = to_m.reshape(total_x * share, XR * n_x * share)
    y_high, y_low = two_parts(along_y)
    x_high, x_low = two_parts(to_m)
    return (
        np.concatenate([y_high, y_low], axis=1),
        np.concatenate([x_high, x_low], axis=0),
        np.concatenate([x_high.T, x_low.T], axis=0),
        np.concatenate([y_high.T, y_high.T, y_low.T], axis=0),
    )


def xy_kernel(planes_ref, scale_ref, y_ref, x_ref, back_x_ref, back_y_ref, out_ref, *, n_x, n_y):
    _, share, block = planes_ref.shape
    total_y = n_y * YC
    lanes = n_y * block
    blocks = planes_ref[...].reshape(n_x, n_y, share, block)
    lines = jnp.concatenate(
        [blocks[:, j].reshape(n_x * share, block) for j in range(n_y)], axis=1
    )
    owner = lax.div(
        lax.rem(lax.broadcasted_iota(jnp.int32, (n_x * share, lanes), 1), jnp.int32(block)),
        jnp.int32(YC),
    )
    stacked = jnp.concatenate([jnp.where(owner == x, lines, 0.0) for x in range(XR)], axis=0)
    high, low = split(stacked)
    pair = mm(high, y_ref[...])
    along_y = pair[:, :total_y] + pair[:, total_y:] + mm(low, y_ref[:, :total_y])

    def along_x(value, table_ref):
        count = table_ref.shape[0] // 2
        both = mm(table_ref[...], jnp.concatenate(split(value), axis=1))
        return both[:count, :total_y] + both[:count, total_y:] + both[count:, :total_y]

    solved = along_x(along_x(along_y, x_ref) * scale_ref[...], back_x_ref)
    high, low = split(solved)
    wide = mm(jnp.concatenate([high, low, high], axis=1), back_y_ref[...])
    span = n_x * share
    lines = wide[:span]
    for x in range(1, XR):
        lines = jnp.where(owner == x, wide[x * span : (x + 1) * span], lines)
    for i in range(n_x):
        for j in range(n_y):
            out_ref[i * n_y + j] = lines[i * share : (i + 1) * share, j * block : (j + 1) * block]


def solve_planes(planes):
    n_x, n_y = lax.axis_size("gx"), lax.axis_size("gy")
    share = planes.shape[0] // (n_x * n_y)
    block = planes.shape[1]
    total_x, total_y = n_x * XR, n_y * YC
    first = (lax.axis_index("gx") * n_y + lax.axis_index("gy")) * share
    scale = influence(
        first + jnp.arange(share, dtype=jnp.int32),
        jnp.arange(total_x, dtype=jnp.int32),
        jnp.arange(total_y, dtype=jnp.int32),
        GZ,
        total_x,
        total_y,
    ) / (total_x * total_y * GZ)
    scale = jnp.swapaxes(scale, 0, 1).reshape(total_x * share, total_y)
    held = planes.reshape(n_x * n_y, share, block)
    held = lax.all_to_all(held, BOTH, split_axis=0, concat_axis=0, tiled=True)
    vmem = pl.BlockSpec(memory_space=pltpu.VMEM)
    held = pl.pallas_call(
        lambda *refs: xy_kernel(*refs, n_x=n_x, n_y=n_y),
        out_shape=jax.ShapeDtypeStruct(held.shape, jnp.float32),
        in_specs=[vmem] * 6,
        out_specs=vmem,
        name="xy_solve",
    )(held, scale, *(jnp.asarray(t) for t in plane_tables(n_x, n_y, share)))
    held = lax.all_to_all(held, BOTH, split_axis=0, concat_axis=0, tiled=True)
    return held.reshape(planes.shape)


def cas_table(length):
    return jnp.asarray(cas_numpy(length).astype(np.float32))


def solve_pencils(planes):
    high = lax.Precision.HIGHEST
    ztrans = planes.reshape(GZ, XR, YC)
    turned = lax.all_to_all(ztrans, "gy", split_axis=0, concat_axis=2, tiled=True)
    total_y = turned.shape[2]
    ytrans = jnp.einsum("zxy,yk->zxk", turned, cas_table(total_y), precision=high)
    turned = lax.all_to_all(ytrans, "gx", split_axis=2, concat_axis=1, tiled=True)
    depth_share, total_x, width_share = turned.shape
    cas_x = cas_table(total_x)
    xtrans = jnp.einsum("zxy,xm->zmy", turned, cas_x, precision=high)
    depth_freq = lax.axis_index("gy") * depth_share + jnp.arange(depth_share, dtype=jnp.int32)
    column_freq = lax.axis_index("gx") * width_share + jnp.arange(width_share, dtype=jnp.int32)
    scale = influence(
        depth_freq, jnp.arange(total_x, dtype=jnp.int32), column_freq, GZ, total_x, total_y
    ) / (total_x * total_y * GZ)
    xback = jnp.einsum("zmy,mx->zxy", xtrans * scale, cas_x, precision=high)
    rows_back = lax.all_to_all(xback, "gx", split_axis=1, concat_axis=2, tiled=True)
    yback = jnp.einsum("zxk,ky->zxy", rows_back, cas_table(total_y), precision=high)
    planes_back = lax.all_to_all(yback, "gy", split_axis=2, concat_axis=0, tiled=True)
    return planes_back.reshape(planes.shape)


def body(positions, charges, cell_index, task_patch, task_near, task_count):
    cas_z = jnp.asarray(np.concatenate(two_parts(cas_numpy(GZ)), axis=0))
    planes = spread_planes(charges, cell_index, cas_z)
    devices = lax.axis_size("gx") * lax.axis_size("gy")
    solve = solve_planes if GZ % (devices * SUBLANES) == 0 else solve_pencils
    planes = solve(planes)
    recip_potential = sample_planes(planes, cell_index, cas_z)

    atoms = jnp.concatenate([positions, charges[None]], axis=0)
    halo = with_halo(atoms, (("gx", 1), ("gy", 2)), 1)
    forces = pair_forces(
        halo, task_patch.reshape(-1), task_near.reshape(-1), task_count.reshape(-1)
    )
    return (forces, recip_potential)


def solution(mesh):
    return jax.shard_map(
        body,
        mesh=mesh,
        in_specs=(
            P(None, "gx", "gy", None),
            P("gx", "gy", None),
            P("gx", "gy", None),
            P("gx", "gy", None),
            P("gx", "gy", None),
            P("gx", "gy"),
        ),
        out_specs=(P(None, "gx", "gy", None), P("gx", "gy", None)),
        check_vma=False,
    )
```

```python
import math

import jax
import jax.numpy as jnp
import numpy as np
from jax import lax
from jax.experimental import pallas as pl
from jax.experimental.pallas import tpu as pltpu
from jax.sharding import PartitionSpec as P

XR = 4
YC = 32
GZ = 256

SCREEN = 72.0
PATCH_SIDE = 12.0
KERNEL_SCALE = 64.0
SUBLANES = 8
BOTH = ("gx", "gy")
SCRATCH = pltpu.CompilerParams(vmem_limit_bytes=16 << 20)


def from_both_sides(first, last, axis):
    count = lax.axis_size(axis)
    up = [(i, (i + 1) % count) for i in range(count)]
    down = [(j, i) for i, j in up]
    return lax.ppermute(last, axis, up), lax.ppermute(first, axis, down)


def halo_edges(positions, charges):
    atoms = [*positions, charges]
    cols = charges.shape[1]
    west, east = from_both_sides(
        jnp.stack([v[:, 0] for v in atoms]),
        jnp.stack([v[:, cols - 1] for v in atoms]),
        "gy",
    )

    def row(r):
        middle = jnp.stack([v[r] for v in atoms])
        return jnp.concatenate([west[:, r : r + 1], middle, east[:, r : r + 1]], axis=1)

    north, south = from_both_sides(row(0), row(charges.shape[0] - 1), "gx")
    return west, east, north, south


def cas_numpy(length):
    steps = np.arange(length)
    angle = (2.0 * math.pi / length) * ((steps[:, None] * steps[None, :]) % length)
    return np.cos(angle) + np.sin(angle)


def two_parts(table):
    table = np.asarray(table, np.float32)
    high = table.astype(jnp.bfloat16)
    low = (table - high.astype(np.float32)).astype(jnp.bfloat16)
    return high, low


def split(value):
    high = value.astype(jnp.bfloat16)
    low = (value - high.astype(jnp.float32)).astype(jnp.bfloat16)
    return high, low


def mm(left, right):
    return jnp.dot(left, right, preferred_element_type=jnp.float32)


def mm_lanes(left, right):
    return lax.dot_general(
        left, right, (((1,), (1,)), ((), ())), preferred_element_type=jnp.float32
    )


def force_kernel(
    patch_ref, near_ref, count_ref, pos_ref, charge_ref, west_ref, east_ref,
    north_ref, south_ref, out_ref, halo_ref,
):
    rows, cols, lanes = charge_ref.shape
    out_ref[...] = jnp.zeros_like(out_ref)
    for c in range(4):
        for r in range(rows):
            own = charge_ref[r] if c == 3 else pos_ref[c, r]
            halo_ref[c, r + 1, 1 : cols + 1, :] = own
            halo_ref[c, r + 1, 0:1, :] = west_ref[c, r : r + 1, :]
            halo_ref[c, r + 1, cols + 1 : cols + 2, :] = east_ref[c, r : r + 1, :]
        halo_ref[c, 0, : cols + 2, :] = north_ref[c]
        halo_ref[c, rows + 1, : cols + 2, :] = south_ref[c]

    def task(t, carry):
        patch = patch_ref[t]
        near = near_ref[t]
        row, col = lax.div(patch, jnp.int32(cols)), lax.rem(patch, jnp.int32(cols))
        drow = lax.div(near, jnp.int32(3)) - 1
        dcol = lax.rem(near, jnp.int32(3)) - 1

        def spot(c, r, s):
            return halo_ref[c, r, pl.ds(s, SUBLANES, stride=0), :]

        first = [spot(c, row + 1, col + 1) for c in range(4)]
        second = [spot(c, row + 1 + drow, col + 1 + dcol) for c in range(4)]
        second[0] = second[0] + drow.astype(jnp.float32) * PATCH_SIDE
        second[1] = second[1] + dcol.astype(jnp.float32) * PATCH_SIDE
        base = [pltpu.roll(v, 0, 1, stride=1, stride_axis=0) for v in second]
        sums = [jnp.zeros((SUBLANES, lanes), jnp.float32) for _ in range(3)]
        for j in range(lanes // SUBLANES):
            other = base if j == 0 else [pltpu.roll(v, j * SUBLANES, 1) for v in base]
            delta = [first[c] - other[c] for c in range(3)]
            dist_sq = delta[0] * delta[0] + delta[1] * delta[1] + delta[2] * delta[2]
            root = lax.rsqrt(dist_sq + 1.0)
            weight = other[3] * jnp.exp(dist_sq * (-1.0 / SCREEN)) * (root * root * root)
            sums = [sums[c] + weight * delta[c] for c in range(3)]
        for c in range(3):
            total = jnp.sum(sums[c], axis=0, keepdims=True) * first[3][:1]
            out_ref[c, row, pl.ds(col, 1), :] = out_ref[c, row, pl.ds(col, 1), :] + total
        return carry

    lax.fori_loop(0, count_ref[0], task, 0)


def pair_forces(positions, charges, patch, near, count):
    rows, cols, atoms = charges.shape
    edges = halo_edges(positions, charges)
    smem = pl.BlockSpec(memory_space=pltpu.SMEM)
    vmem = pl.BlockSpec(memory_space=pltpu.VMEM)
    wide = -(-(cols + 2) // SUBLANES) * SUBLANES + SUBLANES
    return pl.pallas_call(
        force_kernel,
        out_shape=jax.ShapeDtypeStruct(positions.shape, jnp.float32),
        in_specs=[smem] * 3 + [vmem] * 6,
        out_specs=vmem,
        scratch_shapes=[pltpu.VMEM((4, rows + 2, wide, atoms), jnp.float32)],
        compiler_params=SCRATCH,
        name="pair_forces",
    )(patch, near, count, positions, charges, *edges)


def cell_parts(cells, block_cells):
    plane = lax.div(cells, jnp.int32(block_cells))
    return plane, cells - plane * block_cells


def strips(rows, cols):
    deep = rows // XR
    wide = SUBLANES // (YC // cols)
    for strip in range(XR * YC // SUBLANES):
        x, part = divmod(strip, YC // SUBLANES)
        yield strip, [
            (x * deep + a, part * wide + b) for a in range(deep) for b in range(wide)
        ]


def strayed(flat, rows, cols):
    deep = rows // XR
    wide = SUBLANES // (YC // cols)
    row = lax.broadcasted_iota(jnp.int32, flat.shape, 0)
    col = lax.broadcasted_iota(jnp.int32, flat.shape, 1)
    own = lax.div(row, jnp.int32(deep)) * (YC // SUBLANES) + lax.div(col, jnp.int32(wide))
    return jnp.max((lax.div(flat, jnp.int32(SUBLANES)) != own).astype(jnp.int32))


def gather_lanes(value, places):
    return jnp.concatenate([value[r, s : s + 1, :] for r, s in places], axis=1)


def onehot_rows(index, count):
    shape = (count, index.shape[1])
    return (lax.broadcasted_iota(jnp.int32, shape, 0) == index).astype(jnp.bfloat16)


def charge_rows(index, charge, count):
    shape = (count, index.shape[1])
    here = lax.broadcasted_iota(jnp.int32, shape, 0) == index
    high, low = split(jnp.where(here, charge, 0.0))
    return jnp.concatenate([high, low], axis=0)


def spread_kernel(
    charge_hbm, cell_hbm, cas_hbm, out_ref, charge_ref, cell_ref, cas_ref, grid_ref, flat_ref,
    plane_ref, sems,
):
    loads = [
        pltpu.make_async_copy(source, target, sems.at[k])
        for k, (source, target) in enumerate(
            ((charge_hbm, charge_ref), (cell_hbm, cell_ref), (cas_hbm, cas_ref))
        )
    ]
    for load in loads:
        load.start()
    loads[0].wait()
    loads[1].wait()
    rows, cols, _ = charge_ref.shape
    block = out_ref.shape[1]
    depth = out_ref.shape[0]
    charge = charge_ref[...]
    plane, flat = cell_parts(cell_ref[...], block)
    for strip, places in strips(rows, cols):
        index = gather_lanes(flat, places) - strip * SUBLANES
        lines = charge_rows(index, gather_lanes(charge, places), SUBLANES)
        both = mm_lanes(lines, onehot_rows(gather_lanes(plane, places), depth))
        grid_ref[strip * SUBLANES : (strip + 1) * SUBLANES, :] = (
            both[:SUBLANES] + both[SUBLANES:]
        )

    @pl.when(strayed(flat, rows, cols) > 0)
    def _():
        plane_ref[...] = plane.reshape(plane_ref.shape)
        flat_ref[...] = flat.reshape(flat_ref.shape)
        grid_ref[...] = jnp.zeros_like(grid_ref)

        def patch(p, carry):
            row, col = lax.div(p, jnp.int32(cols)), lax.rem(p, jnp.int32(cols))
            lines = charge_rows(
                flat_ref[pl.ds(p, 1), :], charge_ref[row, pl.ds(col, 1), :], block
            )
            both = mm_lanes(lines, onehot_rows(plane_ref[pl.ds(p, 1), :], depth))
            grid_ref[...] = grid_ref[...] + both[:block] + both[block:]
            return carry

        lax.fori_loop(0, rows * cols, patch, 0)

    loads[2].wait()
    high, low = split(grid_ref[...])
    twice = mm_lanes(cas_ref[...], high)
    out_ref[...] = twice[:depth] + twice[depth:] + mm_lanes(cas_ref[:depth], low)


def spread_planes(charges, cells, cas_z):
    rows, cols, atoms = charges.shape
    return pl.pallas_call(
        spread_kernel,
        out_shape=pltpu.VMEM((GZ, XR * YC), jnp.float32),
        in_specs=[pl.BlockSpec(memory_space=pltpu.HBM)] * 3,
        out_specs=pl.BlockSpec(memory_space=pltpu.VMEM),
        scratch_shapes=[
            pltpu.VMEM(charges.shape, charges.dtype),
            pltpu.VMEM(cells.shape, cells.dtype),
            pltpu.VMEM(cas_z.shape, cas_z.dtype),
            pltpu.VMEM((XR * YC, GZ), jnp.float32),
            pltpu.VMEM((rows * cols, atoms), jnp.int32),
            pltpu.VMEM((rows * cols, atoms), jnp.int32),
            pltpu.SemaphoreType.DMA((3,)),
        ],
        compiler_params=SCRATCH,
        name="spread",
    )(*(pltpu.with_memory_space_constraint(v, pltpu.HBM) for v in (charges, cells, cas_z)))


def sample_kernel(planes_ref, cell_ref, cas_ref, out_ref, field_ref, flat_ref, plane_ref):
    rows, cols, _ = cell_ref.shape
    depth, block = planes_ref.shape
    plane, flat = cell_parts(cell_ref[...], block)
    high, low = split(planes_ref[...].T)
    pair = mm(jnp.concatenate([high, low], axis=0), cas_ref[:depth])
    field = pair[:block] + pair[block:] + mm(high, cas_ref[depth:])
    field_high, field_low = split(field)
    for strip, places in strips(rows, cols):
        span = slice(strip * SUBLANES, (strip + 1) * SUBLANES)
        lines = jnp.concatenate([field_high[span], field_low[span]], axis=0)
        both = mm(lines, onehot_rows(gather_lanes(plane, places), depth))
        value = both[:SUBLANES] + both[SUBLANES:]
        index = gather_lanes(flat, places) - strip * SUBLANES
        here = lax.broadcasted_iota(jnp.int32, value.shape, 0) == index
        found = jnp.sum(jnp.where(here, value, 0.0), axis=0, keepdims=True)
        atoms = out_ref.shape[2]
        for k, (r, s) in enumerate(places):
            out_ref[r, s : s + 1, :] = found[:, k * atoms : (k + 1) * atoms]

    @pl.when(strayed(flat, rows, cols) > 0)
    def _():
        plane_ref[...] = plane.reshape(plane_ref.shape)
        flat_ref[...] = flat.reshape(flat_ref.shape)
        field_ref[:block, :] = field_high
        field_ref[block:, :] = field_low

        def patch(p, carry):
            row, col = lax.div(p, jnp.int32(cols)), lax.rem(p, jnp.int32(cols))
            both = mm(field_ref[...], onehot_rows(plane_ref[pl.ds(p, 1), :], depth))
            value = both[:block] + both[block:]
            here = lax.broadcasted_iota(jnp.int32, value.shape, 0) == flat_ref[pl.ds(p, 1), :]
            out_ref[row, pl.ds(col, 1), :] = jnp.sum(
                jnp.where(here, value, 0.0), axis=0, keepdims=True
            )
            return carry

        lax.fori_loop(0, rows * cols, patch, 0)


def sample_planes(planes, cells, cas_z):
    rows, cols, atoms = cells.shape
    vmem = pl.BlockSpec(memory_space=pltpu.VMEM)
    return pl.pallas_call(
        sample_kernel,
        out_shape=jax.ShapeDtypeStruct(cells.shape, jnp.float32),
        in_specs=[vmem] * 3,
        out_specs=vmem,
        scratch_shapes=[
            pltpu.VMEM((2 * XR * YC, GZ), jnp.bfloat16),
            pltpu.VMEM((rows * cols, atoms), jnp.int32),
            pltpu.VMEM((rows * cols, atoms), jnp.int32),
        ],
        compiler_params=SCRATCH,
        name="sample",
    )(planes, cells, cas_z)


def wave_part(freq, length):
    folded = jnp.minimum(freq, length - freq).astype(jnp.float32) / length
    return folded * folded


def influence(depth_freq, row_freq, column_freq, depth_len, row_len, column_len):
    wave_sq = (
        wave_part(depth_freq, depth_len)[:, None, None]
        + wave_part(row_freq, row_len)[None, :, None]
        + wave_part(column_freq, column_len)[None, None, :]
    )
    safe = jnp.where(wave_sq > 0, wave_sq, 1.0)
    return jnp.where(wave_sq > 0, 1.0 / (KERNEL_SCALE * safe), 0.0)


def plane_tables(n_x, n_y, share):
    total_x, total_y = n_x * XR, n_y * YC
    cas_x, cas_y = cas_numpy(total_x), cas_numpy(total_y)
    along_y = np.repeat(cas_y.reshape(n_y, 1, YC, total_y), XR, axis=1)
    along_y = along_y.reshape(n_y * XR * YC, total_y)
    to_m = cas_x.reshape(n_x, XR, total_x).transpose(2, 1, 0)
    to_m = np.einsum("mxi,ab->maxib", to_m, np.eye(share))
    to_m = to_m.reshape(total_x * share, XR * n_x * share)
    y_high, y_low = two_parts(along_y)
    x_high, x_low = two_parts(to_m)
    return (
        np.concatenate([y_high, y_low], axis=1),
        np.concatenate([x_high, x_low], axis=0),
        np.concatenate([x_high.T, x_low.T], axis=0),
        np.concatenate([y_high.T, y_high.T, y_low.T], axis=0),
    )


def xy_kernel(planes_ref, scale_ref, y_ref, x_ref, back_x_ref, back_y_ref, out_ref, *, n_x, n_y):
    _, share, block = planes_ref.shape
    total_y = n_y * YC
    lanes = n_y * block
    blocks = planes_ref[...].reshape(n_x, n_y, share, block)
    lines = jnp.concatenate(
        [blocks[:, j].reshape(n_x * share, block) for j in range(n_y)], axis=1
    )
    owner = lax.div(
        lax.rem(lax.broadcasted_iota(jnp.int32, (n_x * share, lanes), 1), jnp.int32(block)),
        jnp.int32(YC),
    )
    stacked = jnp.concatenate([jnp.where(owner == x, lines, 0.0) for x in range(XR)], axis=0)
    high, low = split(stacked)
    pair = mm(high, y_ref[...])
    along_y = pair[:, :total_y] + pair[:, total_y:] + mm(low, y_ref[:, :total_y])

    def along_x(value, table_ref):
        count = table_ref.shape[0] // 2
        both = mm(table_ref[...], jnp.concatenate(split(value), axis=1))
        return both[:count, :total_y] + both[:count, total_y:] + both[count:, :total_y]

    solved = along_x(along_x(along_y, x_ref) * scale_ref[...], back_x_ref)
    high, low = split(solved)
    wide = mm(jnp.concatenate([high, low, high], axis=1), back_y_ref[...])
    span = n_x * share
    lines = wide[:span]
    for x in range(1, XR):
        lines = jnp.where(owner == x, wide[x * span : (x + 1) * span], lines)
    for i in range(n_x):
        for j in range(n_y):
            out_ref[i * n_y + j] = lines[i * share : (i + 1) * share, j * block : (j + 1) * block]


def solve_planes(planes):
    n_x, n_y = lax.axis_size("gx"), lax.axis_size("gy")
    share = planes.shape[0] // (n_x * n_y)
    block = planes.shape[1]
    total_x, total_y = n_x * XR, n_y * YC
    first = (lax.axis_index("gx") * n_y + lax.axis_index("gy")) * share
    scale = influence(
        first + jnp.arange(share, dtype=jnp.int32),
        jnp.arange(total_x, dtype=jnp.int32),
        jnp.arange(total_y, dtype=jnp.int32),
        GZ,
        total_x,
        total_y,
    ) / (total_x * total_y * GZ)
    scale = jnp.swapaxes(scale, 0, 1).reshape(total_x * share, total_y)
    held = planes.reshape(n_x * n_y, share, block)
    held = lax.all_to_all(held, BOTH, split_axis=0, concat_axis=0, tiled=True)
    vmem = pl.BlockSpec(memory_space=pltpu.VMEM)
    held = pl.pallas_call(
        lambda *refs: xy_kernel(*refs, n_x=n_x, n_y=n_y),
        out_shape=pltpu.VMEM(held.shape, jnp.float32),
        in_specs=[vmem] * 6,
        out_specs=vmem,
        compiler_params=SCRATCH,
        name="xy_solve",
    )(held, scale, *(jnp.asarray(t) for t in plane_tables(n_x, n_y, share)))
    held = lax.all_to_all(held, BOTH, split_axis=0, concat_axis=0, tiled=True)
    return held.reshape(planes.shape)


def cas_table(length):
    return jnp.asarray(cas_numpy(length).astype(np.float32))


def solve_pencils(planes):
    high = lax.Precision.HIGHEST
    ztrans = planes.reshape(GZ, XR, YC)
    turned = lax.all_to_all(ztrans, "gy", split_axis=0, concat_axis=2, tiled=True)
    total_y = turned.shape[2]
    ytrans = jnp.einsum("zxy,yk->zxk", turned, cas_table(total_y), precision=high)
    turned = lax.all_to_all(ytrans, "gx", split_axis=2, concat_axis=1, tiled=True)
    depth_share, total_x, width_share = turned.shape
    cas_x = cas_table(total_x)
    xtrans = jnp.einsum("zxy,xm->zmy", turned, cas_x, precision=high)
    depth_freq = lax.axis_index("gy") * depth_share + jnp.arange(depth_share, dtype=jnp.int32)
    column_freq = lax.axis_index("gx") * width_share + jnp.arange(width_share, dtype=jnp.int32)
    scale = influence(
        depth_freq, jnp.arange(total_x, dtype=jnp.int32), column_freq, GZ, total_x, total_y
    ) / (total_x * total_y * GZ)
    xback = jnp.einsum("zmy,mx->zxy", xtrans * scale, cas_x, precision=high)
    rows_back = lax.all_to_all(xback, "gx", split_axis=1, concat_axis=2, tiled=True)
    yback = jnp.einsum("zxk,ky->zxy", rows_back, cas_table(total_y), precision=high)
    planes_back = lax.all_to_all(yback, "gy", split_axis=2, concat_axis=0, tiled=True)
    return planes_back.reshape(planes.shape)


def whole_planes(devices):
    return GZ % (devices * SUBLANES) == 0


def body(positions, charges, cell_index, task_patch, task_near, task_count):
    cas_z = jnp.asarray(np.concatenate(two_parts(cas_numpy(GZ)), axis=0))
    planes = spread_planes(charges, cell_index, cas_z)
    devices = lax.axis_size("gx") * lax.axis_size("gy")
    planes = (solve_planes if whole_planes(devices) else solve_pencils)(planes)
    recip_potential = sample_planes(planes, cell_index, cas_z)
    forces = pair_forces(
        positions,
        charges,
        task_patch.reshape(-1),
        task_near.reshape(-1),
        task_count.reshape(-1),
    )
    return (forces, recip_potential)


def solution(mesh):
    return jax.shard_map(
        body,
        mesh=mesh,
        in_specs=(
            P(None, "gx", "gy", None),
            P("gx", "gy", None),
            P("gx", "gy", None),
            P("gx", "gy", None),
            P("gx", "gy", None),
            P("gx", "gy"),
        ),
        out_specs=(P(None, "gx", "gy", None), P("gx", "gy", None)),
        check_vma=False,
    )
```

```python
import math

import jax
import jax.numpy as jnp
import numpy as np
from jax import lax
from jax.experimental import pallas as pl
from jax.experimental.pallas import tpu as pltpu
from jax.sharding import PartitionSpec as P

XR = 4
YC = 32
GZ = 256

SCREEN = 72.0
PATCH_SIDE = 12.0
KERNEL_SCALE = 64.0
DECAY = -math.log2(math.e) / SCREEN
TASKS = 2
SUBLANES = 8
SPREAD_CHUNK = 64
SAMPLE_CHUNK = 128
BOTH = ("gx", "gy")
SCRATCH = pltpu.CompilerParams(vmem_limit_bytes=16 << 20)


def from_both_sides(first, last, axis):
    count = lax.axis_size(axis)
    up = [(i, (i + 1) % count) for i in range(count)]
    down = [(j, i) for i, j in up]
    return lax.ppermute(last, axis, up), lax.ppermute(first, axis, down)


def halo_edges(positions, charges):
    atoms = [*positions, charges]
    cols = charges.shape[1]
    west, east = from_both_sides(
        jnp.stack([v[:, 0] for v in atoms]),
        jnp.stack([v[:, cols - 1] for v in atoms]),
        "gy",
    )

    def row(r):
        middle = jnp.stack([v[r] for v in atoms])
        return jnp.concatenate([west[:, r : r + 1], middle, east[:, r : r + 1]], axis=1)

    north, south = from_both_sides(row(0), row(charges.shape[0] - 1), "gx")
    return west, east, north, south


def cas_numpy(length):
    steps = np.arange(length)
    angle = (2.0 * math.pi / length) * ((steps[:, None] * steps[None, :]) % length)
    return np.cos(angle) + np.sin(angle)


def two_parts(table):
    table = np.asarray(table, np.float32)
    high = table.astype(jnp.bfloat16)
    low = (table - high.astype(np.float32)).astype(jnp.bfloat16)
    return high, low


def split(value):
    high = value.astype(jnp.bfloat16)
    low = (value - high.astype(jnp.float32)).astype(jnp.bfloat16)
    return high, low


def mm(left, right):
    return jnp.dot(left, right, preferred_element_type=jnp.float32)


def mm_lanes(left, right):
    return lax.dot_general(
        left, right, (((1,), (1,)), ((), ())), preferred_element_type=jnp.float32
    )


def force_kernel(
    patch_ref, near_ref, count_ref, pos_ref, charge_ref, west_ref, east_ref,
    north_ref, south_ref, out_ref, halo_ref,
):
    rows, cols, lanes = charge_ref.shape
    out_ref[...] = jnp.zeros_like(out_ref)
    for c in range(4):
        for r in range(rows):
            own = charge_ref[r] if c == 3 else pos_ref[c, r]
            halo_ref[c, r + 1, 1 : cols + 1, :] = own
            halo_ref[c, r + 1, 0:1, :] = west_ref[c, r : r + 1, :]
            halo_ref[c, r + 1, cols + 1 : cols + 2, :] = east_ref[c, r : r + 1, :]
        halo_ref[c, 0, : cols + 2, :] = north_ref[c]
        halo_ref[c, rows + 1, : cols + 2, :] = south_ref[c]

    def spot(c, r, s):
        return halo_ref[c, r, pl.ds(s, SUBLANES, stride=0), :]

    def start(t):
        patch, near = patch_ref[0, 0, t], near_ref[0, 0, t]
        row, col = lax.div(patch, jnp.int32(cols)), lax.rem(patch, jnp.int32(cols))
        drow = lax.div(near, jnp.int32(3)) - 1
        dcol = lax.rem(near, jnp.int32(3)) - 1
        first = [spot(c, row + 1, col + 1) for c in range(4)]
        second = [spot(c, row + 1 + drow, col + 1 + dcol) for c in range(4)]
        second[0] = second[0] + drow.astype(jnp.float32) * PATCH_SIDE
        second[1] = second[1] + dcol.astype(jnp.float32) * PATCH_SIDE
        return row, col, first, [pltpu.roll(v, 0, 1, stride=1, stride_axis=0) for v in second]

    def pair(p, carry):
        last = count_ref[0, 0] - 1
        times = [p * TASKS + k for k in range(TASKS)]
        tasks = [start(jnp.minimum(t, last)) for t in times]
        sums = [[jnp.zeros((SUBLANES, lanes), jnp.float32)] * 3 for _ in tasks]
        for j in range(lanes // SUBLANES):
            for k, (_, _, first, base) in enumerate(tasks):
                other = base if j == 0 else [pltpu.roll(v, j * SUBLANES, 1) for v in base]
                delta = [first[c] - other[c] for c in range(3)]
                dist_sq = delta[0] * delta[0] + delta[1] * delta[1] + delta[2] * delta[2]
                root = lax.rsqrt(dist_sq + 1.0)
                weight = other[3] * jnp.exp2(dist_sq * DECAY) * (root * root * root)
                sums[k] = [sums[k][c] + weight * delta[c] for c in range(3)]
        for t, (row, col, first, _), total in zip(times, tasks, sums):
            scale = first[3][:1] * (t <= last).astype(jnp.float32)
            for c in range(3):
                found = jnp.sum(total[c], axis=0, keepdims=True) * scale
                out_ref[c, row, pl.ds(col, 1), :] = out_ref[c, row, pl.ds(col, 1), :] + found
        return carry

    lax.fori_loop(0, lax.div(count_ref[0, 0] + (TASKS - 1), jnp.int32(TASKS)), pair, 0)


def pair_forces(positions, charges, patch, near, count):
    rows, cols, atoms = charges.shape
    edges = halo_edges(positions, charges)
    smem = pl.BlockSpec(memory_space=pltpu.SMEM)
    vmem = pl.BlockSpec(memory_space=pltpu.VMEM)
    wide = -(-(cols + 2) // SUBLANES) * SUBLANES + SUBLANES
    return pl.pallas_call(
        force_kernel,
        out_shape=jax.ShapeDtypeStruct(positions.shape, jnp.float32),
        in_specs=[smem] * 3 + [vmem] * 6,
        out_specs=vmem,
        scratch_shapes=[pltpu.VMEM((4, rows + 2, wide, atoms), jnp.float32)],
        compiler_params=SCRATCH,
        name="pair_forces",
    )(patch, near, count, positions, charges, *edges)


def cell_parts(cells, block_cells):
    plane = lax.div(cells, jnp.int32(block_cells))
    return plane, cells - plane * block_cells


def strips(rows, cols):
    deep = rows // XR
    wide = SUBLANES // (YC // cols)
    for strip in range(XR * YC // SUBLANES):
        x, part = divmod(strip, YC // SUBLANES)
        yield strip, [
            (x * deep + a, part * wide + b) for a in range(deep) for b in range(wide)
        ]


def strayed(flat, rows, cols):
    deep = rows // XR
    wide = SUBLANES // (YC // cols)
    row = lax.broadcasted_iota(jnp.int32, flat.shape, 0)
    col = lax.broadcasted_iota(jnp.int32, flat.shape, 1)
    own = lax.div(row, jnp.int32(deep)) * (YC // SUBLANES) + lax.div(col, jnp.int32(wide))
    return jnp.max((lax.div(flat, jnp.int32(SUBLANES)) != own).astype(jnp.int32))


def gather_lanes(value, places):
    return jnp.concatenate([value[r, s : s + 1, :] for r, s in places], axis=1)


def as_level(index):
    return index.astype(jnp.float32).astype(jnp.bfloat16)


def matches(index, count):
    shape = (count, index.shape[1])
    level = as_level(lax.broadcasted_iota(jnp.int32, (count, 128), 0))
    level = jnp.concatenate([level] * (shape[1] // 128), axis=1)
    return level == jnp.broadcast_to(as_level(index), shape)


def onehot_rows(index, count):
    return jnp.where(matches(index, count), jnp.bfloat16(1), jnp.bfloat16(0))


def charge_rows(index, charge, count):
    here = matches(index, count)
    return jnp.concatenate(
        [jnp.where(here, jnp.broadcast_to(v, here.shape), jnp.bfloat16(0)) for v in split(charge)],
        axis=0,
    )


def spread_kernel(
    charge_hbm, cell_hbm, cas_hbm, out_ref, charge_ref, cell_ref, cas_ref, grid_ref, flat_ref,
    plane_ref, sems,
):
    loads = [
        pltpu.make_async_copy(source, target, sems.at[k])
        for k, (source, target) in enumerate(
            ((charge_hbm, charge_ref), (cell_hbm, cell_ref), (cas_hbm, cas_ref))
        )
    ]
    for load in loads:
        load.start()
    loads[0].wait()
    loads[1].wait()
    rows, cols, _ = charge_ref.shape
    block = out_ref.shape[1]
    depth = out_ref.shape[0]
    charge = charge_ref[...]
    plane, flat = cell_parts(cell_ref[...], block)
    outer, inner = cell_parts(plane, SPREAD_CHUNK)
    chunk = outer * SUBLANES
    tall = depth // SPREAD_CHUNK * SUBLANES
    for strip, places in strips(rows, cols):
        index = gather_lanes(chunk + flat, places) - strip * SUBLANES
        lines = charge_rows(index, gather_lanes(charge, places), tall)
        both = mm_lanes(lines, onehot_rows(gather_lanes(inner, places), SPREAD_CHUNK))
        both = both[:tall] + both[tall:]
        grid_ref[strip * SUBLANES : (strip + 1) * SUBLANES, :] = jnp.concatenate(
            [both[k : k + SUBLANES] for k in range(0, tall, SUBLANES)], axis=1
        )

    @pl.when(strayed(flat, rows, cols) > 0)
    def _():
        plane_ref[...] = plane.reshape(plane_ref.shape)
        flat_ref[...] = flat.reshape(flat_ref.shape)
        grid_ref[...] = jnp.zeros_like(grid_ref)

        def patch(p, carry):
            row, col = lax.div(p, jnp.int32(cols)), lax.rem(p, jnp.int32(cols))
            lines = charge_rows(
                flat_ref[pl.ds(p, 1), :], charge_ref[row, pl.ds(col, 1), :], block
            )
            both = mm_lanes(lines, onehot_rows(plane_ref[pl.ds(p, 1), :], depth))
            grid_ref[...] = grid_ref[...] + both[:block] + both[block:]
            return carry

        lax.fori_loop(0, rows * cols, patch, 0)

    loads[2].wait()
    high, low = split(grid_ref[...])
    twice = mm_lanes(cas_ref[...], high)
    out_ref[...] = twice[:depth] + twice[depth:] + mm_lanes(cas_ref[:depth], low)


def spread_planes(charges, cells, cas_z):
    rows, cols, atoms = charges.shape
    return pl.pallas_call(
        spread_kernel,
        out_shape=pltpu.VMEM((GZ, XR * YC), jnp.float32),
        in_specs=[pl.BlockSpec(memory_space=pltpu.HBM)] * 3,
        out_specs=pl.BlockSpec(memory_space=pltpu.VMEM),
        scratch_shapes=[
            pltpu.VMEM(charges.shape, charges.dtype),
            pltpu.VMEM(cells.shape, cells.dtype),
            pltpu.VMEM(cas_z.shape, cas_z.dtype),
            pltpu.VMEM((XR * YC, GZ), jnp.float32),
            pltpu.VMEM((rows * cols, atoms), jnp.int32),
            pltpu.VMEM((rows * cols, atoms), jnp.int32),
            pltpu.SemaphoreType.DMA((3,)),
        ],
        compiler_params=SCRATCH,
        name="spread",
    )(*(pltpu.with_memory_space_constraint(v, pltpu.HBM) for v in (charges, cells, cas_z)))


def sample_kernel(planes_ref, cell_ref, cas_ref, out_ref, field_ref, flat_ref, plane_ref):
    rows, cols, _ = cell_ref.shape
    depth, block = planes_ref.shape
    plane, flat = cell_parts(cell_ref[...], block)
    high, low = split(planes_ref[...].T)
    pair = mm(jnp.concatenate([high, low], axis=0), cas_ref[:depth])
    field = pair[:block] + pair[block:] + mm(high, cas_ref[depth:])
    outer, inner = cell_parts(plane, SAMPLE_CHUNK)
    chunk = outer * SUBLANES
    tall = depth // SAMPLE_CHUNK * SUBLANES
    for strip, places in strips(rows, cols):
        lines = field[strip * SUBLANES : (strip + 1) * SUBLANES]
        lines = jnp.concatenate(
            [lines[:, k : k + SAMPLE_CHUNK] for k in range(0, depth, SAMPLE_CHUNK)], axis=0
        )
        lines = jnp.concatenate(split(lines), axis=0)
        both = mm(lines, onehot_rows(gather_lanes(inner, places), SAMPLE_CHUNK))
        value = both[:tall] + both[tall:]
        index = gather_lanes(chunk + flat, places) - strip * SUBLANES
        here = lax.broadcasted_iota(jnp.int32, value.shape, 0) == index
        found = jnp.sum(jnp.where(here, value, 0.0), axis=0, keepdims=True)
        atoms = out_ref.shape[2]
        for k, (r, s) in enumerate(places):
            out_ref[r, s : s + 1, :] = found[:, k * atoms : (k + 1) * atoms]

    @pl.when(strayed(flat, rows, cols) > 0)
    def _():
        plane_ref[...] = plane.reshape(plane_ref.shape)
        flat_ref[...] = flat.reshape(flat_ref.shape)
        field_ref[:block, :], field_ref[block:, :] = split(field)

        def patch(p, carry):
            row, col = lax.div(p, jnp.int32(cols)), lax.rem(p, jnp.int32(cols))
            both = mm(field_ref[...], onehot_rows(plane_ref[pl.ds(p, 1), :], depth))
            value = both[:block] + both[block:]
            here = lax.broadcasted_iota(jnp.int32, value.shape, 0) == flat_ref[pl.ds(p, 1), :]
            out_ref[row, pl.ds(col, 1), :] = jnp.sum(
                jnp.where(here, value, 0.0), axis=0, keepdims=True
            )
            return carry

        lax.fori_loop(0, rows * cols, patch, 0)


def sample_planes(planes, cells, cas_z):
    rows, cols, atoms = cells.shape
    vmem = pl.BlockSpec(memory_space=pltpu.VMEM)
    return pl.pallas_call(
        sample_kernel,
        out_shape=jax.ShapeDtypeStruct(cells.shape, jnp.float32),
        in_specs=[vmem] * 3,
        out_specs=vmem,
        scratch_shapes=[
            pltpu.VMEM((2 * XR * YC, GZ), jnp.bfloat16),
            pltpu.VMEM((rows * cols, atoms), jnp.int32),
            pltpu.VMEM((rows * cols, atoms), jnp.int32),
        ],
        compiler_params=SCRATCH,
        name="sample",
    )(planes, cells, cas_z)


def wave_part(freq, length):
    folded = jnp.minimum(freq, length - freq).astype(jnp.float32) / length
    return folded * folded


def influence(depth_freq, row_freq, column_freq, depth_len, row_len, column_len):
    wave_sq = (
        wave_part(depth_freq, depth_len)[:, None, None]
        + wave_part(row_freq, row_len)[None, :, None]
        + wave_part(column_freq, column_len)[None, None, :]
    )
    safe = jnp.where(wave_sq > 0, wave_sq, 1.0)
    return jnp.where(wave_sq > 0, 1.0 / (KERNEL_SCALE * safe), 0.0)


def plane_tables(n_x, n_y, share):
    total_x, total_y = n_x * XR, n_y * YC
    cas_x, cas_y = cas_numpy(total_x), cas_numpy(total_y)
    along_y = np.repeat(cas_y.reshape(n_y, 1, YC, total_y), XR, axis=1)
    along_y = along_y.reshape(n_y * XR * YC, total_y)
    to_m = cas_x.reshape(n_x, XR, total_x).transpose(2, 1, 0)
    to_m = np.einsum("mxi,ab->maxib", to_m, np.eye(share))
    to_m = to_m.reshape(total_x * share, XR * n_x * share)
    y_high, y_low = two_parts(along_y)
    x_high, x_low = two_parts(to_m)
    return (
        np.concatenate([y_high, y_low], axis=1),
        np.concatenate([x_high, x_low], axis=0),
        np.concatenate([x_high.T, x_low.T], axis=0),
        np.concatenate([y_high.T, y_high.T, y_low.T], axis=0),
    )


def xy_kernel(planes_ref, scale_ref, y_ref, x_ref, back_x_ref, back_y_ref, out_ref, *, n_x, n_y):
    _, share, block = planes_ref.shape
    total_y = n_y * YC
    lanes = n_y * block
    blocks = planes_ref[...].reshape(n_x, n_y, share, block)
    lines = jnp.concatenate(
        [blocks[:, j].reshape(n_x * share, block) for j in range(n_y)], axis=1
    )
    owner = lax.div(
        lax.rem(lax.broadcasted_iota(jnp.int32, (n_x * share, lanes), 1), jnp.int32(block)),
        jnp.int32(YC),
    )
    stacked = jnp.concatenate([jnp.where(owner == x, lines, 0.0) for x in range(XR)], axis=0)
    high, low = split(stacked)
    pair = mm(high, y_ref[...])
    along_y = pair[:, :total_y] + pair[:, total_y:] + mm(low, y_ref[:, :total_y])

    def along_x(value, table_ref):
        count = table_ref.shape[0] // 2
        both = mm(table_ref[...], jnp.concatenate(split(value), axis=1))
        return both[:count, :total_y] + both[:count, total_y:] + both[count:, :total_y]

    solved = along_x(along_x(along_y, x_ref) * scale_ref[...], back_x_ref)
    high, low = split(solved)
    wide = mm(jnp.concatenate([high, low, high], axis=1), back_y_ref[...])
    span = n_x * share
    lines = wide[:span]
    for x in range(1, XR):
        lines = jnp.where(owner == x, wide[x * span : (x + 1) * span], lines)
    for i in range(n_x):
        for j in range(n_y):
            out_ref[i * n_y + j] = lines[i * share : (i + 1) * share, j * block : (j + 1) * block]


def solve_planes(planes):
    n_x, n_y = lax.axis_size("gx"), lax.axis_size("gy")
    share = planes.shape[0] // (n_x * n_y)
    block = planes.shape[1]
    total_x, total_y = n_x * XR, n_y * YC
    first = (lax.axis_index("gx") * n_y + lax.axis_index("gy")) * share
    scale = influence(
        first + jnp.arange(share, dtype=jnp.int32),
        jnp.arange(total_x, dtype=jnp.int32),
        jnp.arange(total_y, dtype=jnp.int32),
        GZ,
        total_x,
        total_y,
    ) / (total_x * total_y * GZ)
    scale = jnp.swapaxes(scale, 0, 1).reshape(total_x * share, total_y)
    held = planes.reshape(n_x * n_y, share, block)
    held = lax.all_to_all(held, BOTH, split_axis=0, concat_axis=0, tiled=True)
    vmem = pl.BlockSpec(memory_space=pltpu.VMEM)
    held = pl.pallas_call(
        lambda *refs: xy_kernel(*refs, n_x=n_x, n_y=n_y),
        out_shape=pltpu.VMEM(held.shape, jnp.float32),
        in_specs=[vmem] * 6,
        out_specs=vmem,
        compiler_params=SCRATCH,
        name="xy_solve",
    )(held, scale, *(jnp.asarray(t) for t in plane_tables(n_x, n_y, share)))
    held = lax.all_to_all(held, BOTH, split_axis=0, concat_axis=0, tiled=True)
    return held.reshape(planes.shape)


def cas_table(length):
    return jnp.asarray(cas_numpy(length).astype(np.float32))


def solve_pencils(planes):
    high = lax.Precision.HIGHEST
    ztrans = planes.reshape(GZ, XR, YC)
    turned = lax.all_to_all(ztrans, "gy", split_axis=0, concat_axis=2, tiled=True)
    total_y = turned.shape[2]
    ytrans = jnp.einsum("zxy,yk->zxk", turned, cas_table(total_y), precision=high)
    turned = lax.all_to_all(ytrans, "gx", split_axis=2, concat_axis=1, tiled=True)
    depth_share, total_x, width_share = turned.shape
    cas_x = cas_table(total_x)
    xtrans = jnp.einsum("zxy,xm->zmy", turned, cas_x, precision=high)
    depth_freq = lax.axis_index("gy") * depth_share + jnp.arange(depth_share, dtype=jnp.int32)
    column_freq = lax.axis_index("gx") * width_share + jnp.arange(width_share, dtype=jnp.int32)
    scale = influence(
        depth_freq, jnp.arange(total_x, dtype=jnp.int32), column_freq, GZ, total_x, total_y
    ) / (total_x * total_y * GZ)
    xback = jnp.einsum("zmy,mx->zxy", xtrans * scale, cas_x, precision=high)
    rows_back = lax.all_to_all(xback, "gx", split_axis=1, concat_axis=2, tiled=True)
    yback = jnp.einsum("zxk,ky->zxy", rows_back, cas_table(total_y), precision=high)
    planes_back = lax.all_to_all(yback, "gy", split_axis=2, concat_axis=0, tiled=True)
    return planes_back.reshape(planes.shape)


def whole_planes(devices):
    return GZ % (devices * SUBLANES) == 0


def body(positions, charges, cell_index, task_patch, task_near, task_count):
    cas_z = jnp.asarray(np.concatenate(two_parts(cas_numpy(GZ)), axis=0))
    planes = spread_planes(charges, cell_index, cas_z)
    devices = lax.axis_size("gx") * lax.axis_size("gy")
    planes = (solve_planes if whole_planes(devices) else solve_pencils)(planes)
    recip_potential = sample_planes(planes, cell_index, cas_z)
    forces = pair_forces(
        positions,
        charges,
        task_patch,
        task_near,
        task_count,
    )
    return (forces, recip_potential)


def solution(mesh):
    return jax.shard_map(
        body,
        mesh=mesh,
        in_specs=(
            P(None, "gx", "gy", None),
            P("gx", "gy", None),
            P("gx", "gy", None),
            P("gx", "gy", None),
            P("gx", "gy", None),
            P("gx", "gy"),
        ),
        out_specs=(P(None, "gx", "gy", None), P("gx", "gy", None)),
        check_vma=False,
    )
```
